32 devices in a mesh: dp: 8 (over z, x), mp: 4 (over y, core).
Axes of the slice: x: 2, y: 2, z: 4, core: 2. Of those that a mesh axis runs over, the one named last changes fastest.
Arguments:
- query_emb: bfloat16 [8192, 3584], P('dp', 'mp'), may hold values from -16 to 16
- passage_emb: bfloat16 [16384, 3584], P('dp', 'mp'), may hold values from -4 to 4
- block_ids: int32 [32, 8], P('dp'), may hold values from 0 to 63, as said below
- list_len: int32 [32], P('dp'), may hold values from 2 to 8, as said below
- positive: int32 [8192], P('dp'), may hold values from 0 to 255
Outputs:
- block_scores: bfloat16 [32, 8, 256, 256], P('dp')
- query_loss: float32 [8192], P('dp')
- query_grad: bfloat16 [8192, 3584], P('dp', 'mp')
- passage_grad: bfloat16 [16384, 3584], P('dp', 'mp')
The draws below stay inside these ranges and needn't reach their ends.
Inputs may be any that keep to these rules, and one draw needn't show every extreme that they name: `block_ids`: slot 0 of every query block lists the block that holds its queries' positives. Block id c belongs to owner c // 8. The 32 slots of the query blocks of one index of dp, taken together, name blocks of every owner exactly 4 times. Query block b uses slots 0 to list_len[b] - 1; some query block uses all 8.
All inputs are finite; a program needn't handle non-finite values.
Results may differ from the reference program's by a relative error of at most 0.006.
Values may be sent and summed in bfloat16 or wider, within the bound.
No kernel may reach another device: no remote copies, remote signals or barrier semaphores. Data moves between devices by JAX's collectives and lax.ppermute only.
A program may use at most 192 MiB of HBM per device.

```python
import math
import jax
import jax.numpy as jnp
from jax import lax

D = 3584
BLK = 256
K = 8
QB_DEV = 4
PB_DEV = 8
CAP = 4
NQB = 32
NPB = 64
NQ = 8192
NP = 16384
N_DP = 8


def list_blocks(key):
    device_keys = jax.random.split(jax.random.fold_in(key, 11), N_DP)

    def one_device(device_key):
        first_key, second_key = jax.random.split(device_key)
        owner_list = jnp.tile(jnp.arange(N_DP, dtype=jnp.int32), CAP)
        owner_list = jax.random.permutation(first_key, owner_list)
        local_index = jax.random.randint(second_key, (QB_DEV * K,), 0, PB_DEV, dtype=jnp.int32)
        return owner_list * PB_DEV + local_index
    return jax.vmap(one_device)(device_keys).reshape(NQB, K).astype(jnp.int32)


def joint_floats(key):
    passage_key, query_key = jax.random.split(jax.random.fold_in(key, 37), 2)
    base_passage = jnp.clip(jax.random.normal(passage_key, (NP, D), jnp.float32), -4.0, 4.0)
    base_query = jnp.clip(jax.random.normal(query_key, (NQ, D), jnp.float32), -4.0, 4.0)
    return (base_query, base_passage)


def draw_query_emb(key, part):
    return joint_floats(key)[0].astype(jnp.bfloat16)


def draw_passage_emb(key, part):
    return joint_floats(key)[1].astype(jnp.bfloat16)


def draw_block_ids(key, part):
    return list_blocks(key)


def draw_list_len(key, part):
    first_key, second_key = jax.random.split(jax.random.fold_in(key, 23))
    lengths = jax.random.randint(first_key, (NQB,), 2, K + 1, dtype=jnp.int32)
    fullest = jax.random.randint(second_key, (), 0, NQB, dtype=jnp.int32)
    return lengths.at[fullest].set(K).astype(jnp.int32)


def set_ends(drawn, rng, least, largest):
    extent = drawn.shape
    place = [jax.random.randint(jax.random.fold_in(rng, axis), (), 0, extent[axis]) for axis in range(len(extent))]
    drawn = drawn.at[tuple(place)].set(least)
    longest = extent.index(max(extent))
    place[longest] = (place[longest] + 1) % extent[longest]
    return drawn.at[tuple(place)].set(largest)


def setup_inputs(seed: int = 0) -> dict:
    seeds = jax.random.split(jax.random.key(seed), 6)
    return {
        "query_emb": draw_query_emb(jax.random.fold_in(seeds[5], 71), 0),
        "passage_emb": draw_passage_emb(jax.random.fold_in(seeds[5], 71), 0),
        "block_ids": draw_block_ids(jax.random.fold_in(seeds[5], 71), 0),
        "list_len": draw_list_len(jax.random.fold_in(seeds[5], 71), 0),
        "positive": set_ends(jax.random.randint(seeds[4], (NQ,), 0, BLK), jax.random.fold_in(seeds[4], 1), 0, BLK - 1).astype(jnp.int32),
    }


loss_scale = 64.0

def finish(scores, live_slot, target_col, score_scale):
    keep_mask = live_slot[..., :, None, None]
    masked = jnp.where(keep_mask, scores, jnp.float32(-1e+30))
    row_top = lax.optimization_barrier(jnp.max(masked, axis=(-3, -1), keepdims=True))
    row_total = lax.optimization_barrier(jnp.sum(jnp.exp(masked - row_top), axis=(-3, -1), keepdims=True))
    log_total = row_top + jnp.log(row_total)
    weights = jnp.where(keep_mask, jnp.exp(masked - log_total), jnp.float32(0.0))
    column = lax.broadcasted_iota(jnp.int32, scores.shape, scores.ndim - 1)
    slot_index = lax.broadcasted_iota(jnp.int32, scores.shape, scores.ndim - 3)
    target = ((slot_index == 0) & (column == target_col[..., None, :, None])).astype(jnp.float32)
    query_loss = log_total[..., 0, :, 0] - lax.optimization_barrier(jnp.sum(target * scores, axis=(-3, -1)))
    grad_scores = (loss_scale * score_scale * (weights - target)).astype(jnp.bfloat16)
    shown = jnp.where(keep_mask, scores, jnp.float32(0.0)).astype(jnp.bfloat16)
    return (shown, query_loss, grad_scores)

def reference(query_emb, passage_emb, block_ids, list_len, positive):
    score_scale = 1.0 / math.sqrt(D)
    passage_blocks = passage_emb.reshape(NPB, BLK, D)
    query_blocks = query_emb.reshape(NQB, BLK, D)
    live_all = jnp.arange(K, dtype=jnp.int32)[None, :] < list_len[:, None]
    target_all = positive.reshape(NQB, BLK)

    def one_block(accumulated, carried):
        query_rows, slot_ids, live_slot, target_col = carried
        listed = passage_blocks[slot_ids]
        scores = jnp.einsum('id,kjd->kij', query_rows.astype(jnp.float32), listed.astype(jnp.float32)) * score_scale
        shown, query_loss, grad_scores = finish(scores, live_slot, target_col, score_scale)
        grad_float = grad_scores.astype(jnp.float32)
        query_grad = jnp.einsum('kij,kjd->id', grad_float, listed.astype(jnp.float32)).astype(jnp.bfloat16)
        slot_terms = jnp.einsum('kij,id->kjd', grad_float, query_rows.astype(jnp.float32)).astype(jnp.bfloat16)
        accumulated = accumulated.at[slot_ids].add(slot_terms.astype(jnp.float32))
        return (accumulated, (shown, query_loss, query_grad))
    initial = jnp.zeros((NPB, BLK, D), jnp.float32)
    accumulated, (shown, query_loss, query_grad) = lax.scan(one_block, initial, (query_blocks, block_ids, live_all, target_all))
    return (shown, query_loss.reshape(NQ), query_grad.reshape(NQ, D), accumulated.astype(jnp.bfloat16).reshape(NP, D))
```

```python
import functools
import math

import jax
import jax.numpy as jnp
from jax import lax
from jax.experimental import pallas as pl
from jax.experimental.pallas import tpu as pltpu
from jax.sharding import PartitionSpec as P

D = 3584
BLK = 256
HALVES = 2
LOSS_SCALE = 64.0
SCORE_SCALE = 1.0 / math.sqrt(D)
LOW = -1e30
LANES = 128
VMEM_LIMIT = 56 * 1024 * 1024


F_BLOCK, F_SLOT, F_LIVE, F_PASS = range(4)


def params(**kw):
    return pltpu.CompilerParams(vmem_limit_bytes=VMEM_LIMIT, **kw)


ANY = pl.BlockSpec(memory_space=pl.ANY)
SMEM = pl.BlockSpec(memory_space=pltpu.SMEM)
VMEM = pl.BlockSpec(memory_space=pltpu.VMEM)


class Plan:
    def __init__(self, rows, cols, mp, query_blocks, slots, pass_blocks, width):
        self.A, self.B, self.M = rows, cols, mp
        self.J, self.K, self.PB, self.W = query_blocks, slots, pass_blocks, width
        self.CAP = query_blocks * slots // (rows * cols)
        self.PAIRS = self.B * self.CAP
        self.R = BLK // HALVES
        self.RM = self.R // mp

    def field(self, tab, field, s, q):
        row = lax.rem(tab[4 * self.A * self.PAIRS] + (self.A - s), self.A)
        return tab[(field * self.A + row) * self.PAIRS + q]

    def column(self, tab, s, q):
        row = lax.rem(tab[4 * self.A * self.PAIRS] + (self.A - s), self.A)
        return row * self.J + tab[row * self.PAIRS + q]


def score_kernel(g, steps, shifts, tab, *refs):
    nq, nt = len(steps), len(shifts)
    q_refs, p_refs = refs[:nq], refs[nq : nq + nt]
    out, q_buf, p_buf, q_sem, p_sem = refs[nq + nt :]
    per = nt * g.CAP

    for i in range(nq):
        pltpu.make_async_copy(q_refs[i], q_buf.at[i], q_sem.at[i]).start()
    for i, s in enumerate(steps):
        for n, t in enumerate(shifts):

            def fetch(c, carry):
                at = i * per + n * g.CAP + c
                src = p_refs[n].at[g.field(tab, F_PASS, s, t * g.CAP + c)]
                pltpu.make_async_copy(src, p_buf.at[at], p_sem.at[at]).start()
                return carry

            lax.fori_loop(0, g.CAP, fetch, 0)
    for i, s in enumerate(steps):
        pltpu.make_async_copy(q_refs[i], q_buf.at[i], q_sem.at[i]).wait()
        for n, t in enumerate(shifts):

            def pair(c, carry):
                at = i * per + n * g.CAP + c
                pltpu.make_async_copy(p_refs[n].at[0], p_buf.at[at], p_sem.at[at]).wait()
                q = q_buf[i, g.field(tab, F_BLOCK, s, t * g.CAP + c)]
                part = lax.dot_general(
                    q, p_buf[at], (((1,), (1,)), ((), ())), preferred_element_type=jnp.float32
                )
                out[:, at] = part.reshape(g.M, g.RM, BLK)
                return carry

            lax.fori_loop(0, g.CAP, pair, 0)


def scores(g, tab, queries, passages, steps, shifts):
    nq, nt = len(steps), len(shifts)
    n = nq * nt * g.CAP
    return pl.pallas_call(
        functools.partial(score_kernel, g, steps, shifts),
        out_shape=jax.ShapeDtypeStruct((g.M, n, g.RM, BLK), jnp.float32),
        in_specs=[SMEM] + [ANY] * (nq + nt),
        out_specs=VMEM,
        scratch_shapes=[
            pltpu.VMEM((nq, g.J, g.R, g.W), jnp.bfloat16),
            pltpu.VMEM((n, BLK, g.W), jnp.bfloat16),
            pltpu.SemaphoreType.DMA((nq,)),
            pltpu.SemaphoreType.DMA((n,)),
        ],
        compiler_params=params(),
        cost_estimate=pl.CostEstimate(
            flops=2 * n * g.R * BLK * g.W,
            bytes_accessed=n * BLK * g.W * 2 + nq * g.J * g.R * g.W * 2 + n * g.R * BLK * 4,
            transcendentals=0,
        ),
        name="scores",
    )(tab, *[queries[s] for s in steps], *[passages[t] for t in shifts])


def lane_pick(values, at):
    lane = lax.broadcasted_iota(jnp.int32, values.shape, 1)
    return jnp.sum(jnp.where(lane == at, values, jnp.zeros_like(values)), axis=1, keepdims=True)


def stats_kernel(g, groups, tab, positive, *refs):
    ng = len(groups)
    score_refs = refs[:ng]
    stats = refs[ng]
    shown = refs[ng + 1 :]
    lane = lax.broadcasted_iota(jnp.int32, (g.RM, LANES), 1)
    col = lax.broadcasted_iota(jnp.int32, (g.RM, BLK), 1)
    carry = (
        jnp.full((g.RM, LANES), LOW, jnp.float32),
        jnp.zeros((g.RM, LANES), jnp.float32),
        jnp.zeros((g.RM, LANES), jnp.float32),
    )
    for i, (steps, shifts) in enumerate(groups):
        for a, s in enumerate(steps):
            for b, t in enumerate(shifts):

                def pair(c, carry):
                    top, total, hit = carry
                    q = t * g.CAP + c
                    live = g.field(tab, F_LIVE, s, q)
                    first = g.field(tab, F_SLOT, s, q) == 0
                    at = g.column(tab, s, q)
                    x = score_refs[i][(a * len(shifts) + b) * g.CAP + c] * SCORE_SCALE
                    shown[s][q] = jnp.where(live > 0, x, 0.0).astype(jnp.bfloat16)
                    here = (lane == at) & (live > 0)
                    row_top = jnp.max(x, axis=1, keepdims=True)
                    row_sum = jnp.sum(jnp.exp(x - row_top), axis=1, keepdims=True)
                    new_top = jnp.where(here, jnp.maximum(top, row_top), top)
                    grown = total * jnp.exp(top - new_top) + row_sum * jnp.exp(row_top - new_top)
                    total = jnp.where(here, grown, total)
                    pos = lane_pick(positive[...], at)
                    mine = jnp.sum(jnp.where((col == pos) & first, x, 0.0), axis=1, keepdims=True)
                    hit = jnp.where(lane == at, hit + mine, hit)
                    return new_top, total, hit

                carry = lax.fori_loop(0, g.CAP, pair, carry)
    for n in range(3):
        stats[n] = carry[n]


def stats_of(g, tab, positive, score_list, groups):
    return pl.pallas_call(
        functools.partial(stats_kernel, g, groups),
        out_shape=[jax.ShapeDtypeStruct((3, g.RM, LANES), jnp.float32)]
        + [jax.ShapeDtypeStruct((g.PAIRS, g.RM, BLK), jnp.bfloat16)] * g.A,
        in_specs=[SMEM, VMEM] + [VMEM] * len(groups),
        out_specs=[VMEM] * (1 + g.A),
        compiler_params=params(),
        cost_estimate=pl.CostEstimate(
            flops=g.A * g.PAIRS * g.RM * BLK * 8,
            bytes_accessed=g.A * g.PAIRS * g.RM * BLK * 6,
            transcendentals=g.A * g.PAIRS * g.RM * BLK,
        ),
        name="stats",
    )(tab, positive, *score_list)


def grad_kernel(g, groups, tab, positive, stats, *refs):
    ng = len(groups)
    score_refs = refs[:ng]
    loss = refs[ng]
    grads = refs[ng + 1 :]
    col = lax.broadcasted_iota(jnp.int32, (g.RM, BLK), 1)
    top = stats[0, 0]
    for n in range(1, g.A):
        top = jnp.maximum(top, stats[n, 0])
    total = jnp.zeros((g.RM, LANES), jnp.float32)
    hit = jnp.zeros((g.RM, LANES), jnp.float32)
    for n in range(g.A):
        total = total + stats[n, 1] * jnp.exp(stats[n, 0] - top)
        hit = hit + stats[n, 2]
    log_total = top + jnp.log(total)
    loss[...] = log_total - hit
    for i, (steps, shifts) in enumerate(groups):
        for a, s in enumerate(steps):
            for b, t in enumerate(shifts):

                def pair(c, carry):
                    q = t * g.CAP + c
                    live = g.field(tab, F_LIVE, s, q)
                    first = g.field(tab, F_SLOT, s, q) == 0
                    at = g.column(tab, s, q)
                    x = score_refs[i][(a * len(shifts) + b) * g.CAP + c] * SCORE_SCALE
                    weight = jnp.exp(x - lane_pick(log_total, at))
                    pos = lane_pick(positive[...], at)
                    target = jnp.where((col == pos) & first, 1.0, 0.0)
                    grad = LOSS_SCALE * SCORE_SCALE * (weight - target)
                    grads[s][q] = jnp.where(live > 0, grad, 0.0).astype(jnp.bfloat16)
                    return carry

                lax.fori_loop(0, g.CAP, pair, 0)


def grads_of(g, tab, positive, stats, score_list, groups):
    return pl.pallas_call(
        functools.partial(grad_kernel, g, groups),
        out_shape=[jax.ShapeDtypeStruct((g.RM, LANES), jnp.float32)]
        + [jax.ShapeDtypeStruct((g.PAIRS, g.RM, BLK), jnp.bfloat16)] * g.A,
        in_specs=[SMEM, VMEM, VMEM] + [VMEM] * len(groups),
        out_specs=[VMEM] * (1 + g.A),
        compiler_params=params(),
        cost_estimate=pl.CostEstimate(
            flops=g.A * g.PAIRS * g.RM * BLK * 8,
            bytes_accessed=g.A * g.PAIRS * g.RM * BLK * 6,
            transcendentals=g.A * g.PAIRS * g.RM * BLK,
        ),
        name="grads",
    )(tab, positive, stats, *score_list)


def query_grad_kernel(g, s, tab, grad, *refs):
    p_refs = refs[: g.B]
    out, acc, p_buf, p_sem = refs[g.B :]
    for t in range(g.B):

        def fetch(c, carry):
            at = t * g.CAP + c
            src = p_refs[t].at[g.field(tab, F_PASS, s, at)]
            pltpu.make_async_copy(src, p_buf.at[at], p_sem.at[at]).start()
            return carry

        lax.fori_loop(0, g.CAP, fetch, 0)
    acc[...] = jnp.zeros_like(acc)

    def pair(at, carry):
        pltpu.make_async_copy(p_refs[0].at[0], p_buf.at[at], p_sem.at[at]).wait()
        j = g.field(tab, F_BLOCK, s, at)
        rows = grad[:, at].reshape(g.R, BLK)
        acc[j] += jnp.dot(rows, p_buf[at], preferred_element_type=jnp.float32)
        return carry

    lax.fori_loop(0, g.PAIRS, pair, 0)
    out[...] = acc[...].astype(out.dtype)


def query_grad_part(g, tab, grad, passages, s, dtype):
    return pl.pallas_call(
        functools.partial(query_grad_kernel, g, s),
        out_shape=jax.ShapeDtypeStruct((g.J, g.R, g.W), dtype),
        in_specs=[SMEM, VMEM] + [ANY] * g.B,
        out_specs=VMEM,
        scratch_shapes=[
            pltpu.VMEM((g.J, g.R, g.W), jnp.float32),
            pltpu.VMEM((g.PAIRS, BLK, g.W), jnp.bfloat16),
            pltpu.SemaphoreType.DMA((g.PAIRS,)),
        ],
        compiler_params=params(),
        cost_estimate=pl.CostEstimate(
            flops=2 * g.PAIRS * g.R * BLK * g.W,
            bytes_accessed=g.PAIRS * BLK * g.W * 2 + g.J * g.R * g.W * 4,
            transcendentals=0,
        ),
        name="query_grad_part",
    )(tab, grad, *passages)


def passage_grad_kernel(g, t, tab, *refs):
    n = g.A * HALVES
    grads, q_refs = refs[:n], refs[n : 2 * n]
    out, acc, g_buf, q_buf, g_sem, q_sem = refs[2 * n :]

    def copies(i):
        yield pltpu.make_async_copy(
            grads[i].at[:, pl.ds(t * g.CAP, g.CAP)], g_buf.at[i], g_sem.at[i]
        )
        yield pltpu.make_async_copy(q_refs[i], q_buf.at[i], q_sem.at[i])

    for i in range(n):
        for copy in copies(i):
            copy.start()
    acc[...] = jnp.zeros_like(acc)
    for s in range(g.A):
        for h in range(HALVES):
            for copy in copies(s * HALVES + h):
                copy.wait()

        def pair(c, carry):
            q = t * g.CAP + c
            j = g.field(tab, F_BLOCK, s, q)
            block = g.field(tab, F_PASS, s, q)
            term = jnp.zeros((BLK, g.W), jnp.float32)
            for h in range(HALVES):
                i = s * HALVES + h
                rows = g_buf[i, :, c].reshape(g.R, BLK)
                term += lax.dot_general(
                    rows, q_buf[i, j], (((0,), (0,)), ((), ())), preferred_element_type=jnp.float32
                )
            acc[block] += term.astype(jnp.bfloat16).astype(jnp.float32)
            return carry

        lax.fori_loop(0, g.CAP, pair, 0)
    out[...] = acc[...].astype(out.dtype)


def passage_grad_part(g, tab, grads, queries, t, dtype):
    n = g.A * HALVES
    return pl.pallas_call(
        functools.partial(passage_grad_kernel, g, t),
        out_shape=jax.ShapeDtypeStruct((g.PB, BLK, g.W), dtype),
        in_specs=[SMEM] + [ANY] * (2 * n),
        out_specs=VMEM,
        scratch_shapes=[
            pltpu.VMEM((g.PB, BLK, g.W), jnp.float32),
            pltpu.VMEM((n, g.M, g.CAP, g.RM, BLK), jnp.bfloat16),
            pltpu.VMEM((n, g.J, g.R, g.W), jnp.bfloat16),
            pltpu.SemaphoreType.DMA((n,)),
            pltpu.SemaphoreType.DMA((n,)),
        ],
        compiler_params=params(),
        cost_estimate=pl.CostEstimate(
            flops=2 * g.A * g.CAP * BLK * BLK * g.W,
            bytes_accessed=g.A * g.J * BLK * g.W * 2 + g.PB * BLK * g.W * 4,
            transcendentals=0,
        ),
        name="passage_grad_part",
    )(tab, *grads, *queries)


def place_kernel(g, where, src, out):
    def slot(i, carry):
        w = where[i]
        s, q = lax.div(w, g.PAIRS), lax.rem(w, g.PAIRS)
        for h in range(HALVES):
            out[i, pl.ds(h * g.R, g.R)] = src[:, h, s, q].reshape(g.R, BLK)
        return carry

    lax.fori_loop(0, g.J * g.K, slot, 0)


def place(g, where, gathered):
    return pl.pallas_call(
        functools.partial(place_kernel, g),
        out_shape=jax.ShapeDtypeStruct((g.J * g.K, BLK, BLK), jnp.bfloat16),
        in_specs=[SMEM, VMEM],
        out_specs=VMEM,
        compiler_params=params(),
        cost_estimate=pl.CostEstimate(
            flops=0, bytes_accessed=2 * g.J * g.K * BLK * BLK * 2, transcendentals=0
        ),
        name="place",
    )(where, gathered)


def grid_of(count):
    cols = 2 ** (int(math.log2(count)) // 2)
    return count // cols, cols


def shards(query_emb, passage_emb, block_ids, list_len, positive):
    count = lax.axis_size("dp")
    rows, cols = grid_of(count)
    width = query_emb.shape[1]
    g = Plan(
        rows, cols, lax.axis_size("mp"), block_ids.shape[0], block_ids.shape[1],
        passage_emb.shape[0] // BLK, width,
    )
    A, B, J, K = g.A, g.B, g.J, g.K
    ring = [(a * B + b, (a + 1) % A * B + b) for a in range(A) for b in range(B)]
    along = [[a * B + b for a in range(A)] for b in range(B)]

    def back(s):
        return [(a * B + b, (a - s) % A * B + b) for a in range(A) for b in range(B)]

    def turn(t):
        return [(a * B + b, a * B + (b + t) % B) for a in range(A) for b in range(B)]

    me = lax.axis_index("dp")
    row, column = me // B, me % B

    own_q = query_emb.reshape(J, HALVES, g.R, width)
    own_p = passage_emb.reshape(g.PB, BLK, width)
    passages = [own_p] + [lax.ppermute(own_p, "dp", turn(B - t)) for t in range(1, B)]
    queries = []
    held = None
    for h in range(HALVES):
        now = own_q[:, h]
        if held is not None:
            now, _ = lax.optimization_barrier((now, held))
        ringed = [now]
        for s in range(1, A):
            ringed.append(lax.ppermute(ringed[-1], "dp", ring))
        held = ringed[max(A - 2, 0)]
        queries.append(ringed)

    info = jnp.concatenate([block_ids, list_len[:, None], positive.reshape(J, BLK)], axis=1)
    info = lax.all_gather(info, "dp", axis_index_groups=along)
    ids = info[:, :, :K].reshape(A, J * K)
    lens = info[:, :, K]
    owner = ids // g.PB
    order = jnp.arange(J * K, dtype=jnp.int32)
    earlier = (owner[:, :, None] == owner[:, None, :]) & (order[None, None, :] < order[None, :, None])
    rank = jnp.sum(earlier.astype(jnp.int32), axis=2)
    place_of = (owner % B + B - column) % B * g.CAP + rank
    mine = jnp.where(owner // B == row, place_of, -1)
    hot = mine[:, None, :] == jnp.arange(g.PAIRS, dtype=jnp.int32)[None, :, None]
    live = order[None, :] % K < jnp.repeat(lens, K, axis=1)

    def pick(values):
        return jnp.sum(jnp.where(hot, values[:, None, :], 0), axis=2)

    fields = [
        pick(jnp.broadcast_to(order // K, ids.shape)),
        pick(jnp.broadcast_to(order % K, ids.shape)),
        pick(live.astype(jnp.int32)),
        pick(ids % g.PB),
    ]
    tab = jnp.concatenate([jnp.stack(fields).reshape(-1), row.reshape(1)])
    own_owner = lax.dynamic_index_in_dim(owner, row, 0, keepdims=False)
    own_place = lax.dynamic_index_in_dim(place_of, row, 0, keepdims=False)
    where = (own_owner // B + A - row) % A * g.PAIRS + own_place

    m = lax.axis_index("mp")
    lanes = info[:, :, K + 1 :].reshape(A * J, HALVES, g.M, g.RM)
    lanes = lax.dynamic_index_in_dim(lanes, m, 2, keepdims=False).transpose(1, 2, 0)
    lanes = jnp.pad(lanes, ((0, 0), (0, 0), (0, LANES - A * J)))

    every = tuple(range(A))
    shifts = tuple(range(B))
    grads, losses, seen = [], [], []
    for h in range(HALVES):
        if h == 0 and HALVES > 1:
            groups = [(every, (0,)), (every, shifts[1:])]
        else:
            groups = [(every[:-1], shifts), (every[-1:], shifts)]
        score_list = [
            lax.psum_scatter(scores(g, tab, queries[h], passages, s, t), "mp", scatter_dimension=0)
            for s, t in groups
        ]
        stats, *shown = stats_of(g, tab, lanes[h], score_list, groups)
        stats = lax.all_gather(stats, "dp", axis_index_groups=along)
        loss, *grad = grads_of(g, tab, lanes[h], stats, score_list, groups)
        grads.append([lax.all_gather(grad[s], "mp") for s in (*range(1, A), 0)])
        grads[-1] = grads[-1][-1:] + grads[-1][:-1]
        losses.append(loss)
        seen.append([shown[0]] + [lax.ppermute(shown[s], "dp", back(s)) for s in range(1, A)])

    out_q = []
    for h in range(HALVES):
        total = query_grad_part(g, tab, grads[h][1 % A], passages, 1 % A, jnp.bfloat16)
        for s in [*range(2, A), 0]:
            part = query_grad_part(g, tab, grads[h][s], passages, s, jnp.float32)
            total = lax.ppermute(total, "dp", ring)
            total = (part + total.astype(jnp.float32)).astype(jnp.bfloat16)
        out_q.append(total)
    query_grad = jnp.stack(out_q, axis=1).reshape(J * BLK, width)

    flat_g = [grads[h][s] for s in range(A) for h in range(HALVES)]
    flat_q = [queries[h][s] for s in range(A) for h in range(HALVES)]
    sent = [
        lax.ppermute(passage_grad_part(g, tab, flat_g, flat_q, t, jnp.bfloat16), "dp", turn(t))
        for t in range(1, B)
    ]
    total = passage_grad_part(g, tab, flat_g, flat_q, 0, jnp.float32)
    for part in sent:
        total = total + part.astype(jnp.float32)
    passage_grad = total.astype(jnp.bfloat16).reshape(g.PB * BLK, width)

    shown = jnp.stack([jnp.stack(list(part)) for part in seen])
    shown = lax.all_gather(shown, "mp")
    block_scores = place(g, where, shown).reshape(J, K, BLK, BLK)
    loss = lax.dynamic_slice_in_dim(jnp.stack(losses), row * J, J, 2)
    loss = lax.all_gather(loss, "mp")
    query_loss = loss.transpose(3, 1, 0, 2).reshape(J * BLK)
    return block_scores, query_loss, query_grad, passage_grad


def solution(mesh):
    return jax.shard_map(
        shards,
        mesh=mesh,
        in_specs=(P("dp", "mp"), P("dp", "mp"), P("dp", None), P("dp"), P("dp")),
        out_specs=(P("dp", None, None, None), P("dp"), P("dp", "mp"), P("dp", "mp")),
        check_vma=False,
    )
```

```python
import functools
import math

import jax
import jax.numpy as jnp
from jax import lax
from jax.experimental import pallas as pl
from jax.experimental.pallas import tpu as pltpu
from jax.sharding import PartitionSpec as P


D = 3584
BLK = 256
HALVES = 2
LOSS_SCALE = 64.0
SCORE_SCALE = 1.0 / math.sqrt(D)
LOW = -1e30
LANES = 128
PART = LANES // 4
VMEM_LIMIT = 56 * 1024 * 1024


F_BLOCK, F_SLOT, F_LIVE, F_PASS = range(4)


def params(**kw):
    return pltpu.CompilerParams(vmem_limit_bytes=VMEM_LIMIT, **kw)


ANY = pl.BlockSpec(memory_space=pl.ANY)
SMEM = pl.BlockSpec(memory_space=pltpu.SMEM)
VMEM = pl.BlockSpec(memory_space=pltpu.VMEM)


class Plan:
    def __init__(self, rows, cols, mp, query_blocks, slots, pass_blocks, width):
        self.A, self.B, self.M = rows, cols, mp
        self.J, self.K, self.PB, self.W = query_blocks, slots, pass_blocks, width
        self.CAP = query_blocks * slots // (rows * cols)
        self.PAIRS = self.B * self.CAP
        self.R = BLK // HALVES
        self.RM = self.R // mp

    def field(self, tab, field, s, q):
        return tab[(field * self.A + s) * self.PAIRS + q]

    def rest(self, s):
        return (s - 2) % self.A

    def column(self, tab, s, q):
        row = lax.rem(tab[4 * self.A * self.PAIRS] + (self.A - s), self.A)
        return row * self.J + tab[s * self.PAIRS + q]


def score_kernel(g, combos, tab, *refs):
    steps = sorted({s for s, _ in combos})
    shifts = sorted({t for _, t in combos})
    nq, nt = len(steps), len(shifts)
    q_refs, p_refs = refs[:nq], refs[nq : nq + nt]
    out, q_buf, p_buf, q_sem, p_sem = refs[nq + nt :]

    for i in range(nq):
        pltpu.make_async_copy(q_refs[i], q_buf.at[i], q_sem.at[i]).start()
    spans = []
    for n, (s, t) in enumerate(combos):
        if spans and spans[-1][0] == t and spans[-1][2] == s:
            spans[-1][2] = s + 1
        else:
            spans.append([t, s, s + 1, n - s])
    for t, low, high, base in spans:

        def fetch(s, carry):
            for c in range(g.CAP):
                at = (base + s) * g.CAP + c
                src = p_refs[shifts.index(t)].at[g.field(tab, F_PASS, s, t * g.CAP + c)]
                pltpu.make_async_copy(src, p_buf.at[at], p_sem.at[at]).start()
            return carry

        lax.fori_loop(low, high, fetch, 0)
    for i in range(nq):
        pltpu.make_async_copy(q_refs[i], q_buf.at[i], q_sem.at[i]).wait()
    for t, low, high, base in spans:

        def pairs(s, carry):
            for c in range(g.CAP):
                at = (base + s) * g.CAP + c
                pltpu.make_async_copy(p_refs[0].at[0], p_buf.at[at], p_sem.at[at]).wait()
                q = q_buf[s - steps[0], g.field(tab, F_BLOCK, s, t * g.CAP + c)]
                part = lax.dot_general(
                    q, p_buf[at], (((1,), (1,)), ((), ())), preferred_element_type=jnp.float32
                )
                out[:, at] = part.reshape(g.M, g.RM, BLK)
            return carry

        lax.fori_loop(low, high, pairs, 0)


def scores(g, tab, queries, passages, combos):
    steps = sorted({s for s, _ in combos})
    shifts = sorted({t for _, t in combos})
    nq, nt = len(steps), len(shifts)
    n = len(combos) * g.CAP
    return pl.pallas_call(
        functools.partial(score_kernel, g, combos),
        out_shape=jax.ShapeDtypeStruct((g.M, n, g.RM, BLK), jnp.float32),
        in_specs=[SMEM] + [ANY] * (nq + nt),
        out_specs=VMEM,
        scratch_shapes=[
            pltpu.VMEM((nq, g.J, g.R, g.W), jnp.bfloat16),
            pltpu.VMEM((n, BLK, g.W), jnp.bfloat16),
            pltpu.SemaphoreType.DMA((nq,)),
            pltpu.SemaphoreType.DMA((n,)),
        ],
        compiler_params=params(),
        cost_estimate=pl.CostEstimate(
            flops=2 * n * g.R * BLK * g.W,
            bytes_accessed=n * BLK * g.W * 2 + nq * g.J * g.R * g.W * 2 + n * g.R * BLK * 4,
            transcendentals=0,
        ),
        name="scores",
    )(tab, *[queries[s] for s in steps], *[passages[t] for t in shifts])


def lane_pick(values, at):
    lane = lax.broadcasted_iota(jnp.int32, values.shape, 1)
    return jnp.sum(jnp.where(lane == at, values, jnp.zeros_like(values)), axis=1, keepdims=True)


def stats_kernel(g, groups, tab, positive, *refs):
    ng = len(groups)
    score_refs = refs[:ng]
    stats = refs[ng]
    shown = refs[ng + 1 :]
    lane = lax.broadcasted_iota(jnp.int32, (g.RM, LANES), 1)
    col = lax.broadcasted_iota(jnp.int32, (g.RM, BLK), 1)
    carry = (
        jnp.full((g.RM, LANES), LOW, jnp.float32),
        jnp.zeros((g.RM, LANES), jnp.float32),
        jnp.zeros((g.RM, LANES), jnp.float32),
    )
    for i, combos in enumerate(groups):
        for n, (s, t) in enumerate(combos):
            for c in range(g.CAP):

                def pair(carry):
                    top, total, hit = carry
                    q = t * g.CAP + c
                    live = g.field(tab, F_LIVE, s, q)
                    first = g.field(tab, F_SLOT, s, q) == 0
                    at = g.column(tab, s, q)
                    x = score_refs[i][n * g.CAP + c] * SCORE_SCALE
                    shown[s][q] = jnp.where(live > 0, x, 0.0).astype(jnp.bfloat16)
                    here = (lane == at) & (live > 0)
                    row_top = jnp.max(x, axis=1, keepdims=True)
                    row_sum = jnp.sum(jnp.exp(x - row_top), axis=1, keepdims=True)
                    new_top = jnp.where(here, jnp.maximum(top, row_top), top)
                    grown = total * jnp.exp(top - new_top) + row_sum * jnp.exp(row_top - new_top)
                    total = jnp.where(here, grown, total)
                    pos = lane_pick(positive[...], s * g.J + g.field(tab, F_BLOCK, s, q))
                    mine = jnp.sum(jnp.where((col == pos) & first, x, 0.0), axis=1, keepdims=True)
                    hit = jnp.where(lane == at, hit + mine, hit)
                    return new_top, total, hit

                carry = pair(carry)
    top, total, hit = carry
    packed = jnp.where(lane < PART, top, pltpu.roll(total, PART, 1))
    stats[...] = jnp.where(lane < 2 * PART, packed, pltpu.roll(hit, 2 * PART, 1))


def stats_of(g, tab, positive, score_list, groups):
    return pl.pallas_call(
        functools.partial(stats_kernel, g, groups),
        out_shape=[jax.ShapeDtypeStruct((g.RM, LANES), jnp.float32)]
        + [jax.ShapeDtypeStruct((g.PAIRS, g.RM, BLK), jnp.bfloat16)] * g.A,
        in_specs=[SMEM, VMEM] + [VMEM] * len(groups),
        out_specs=[VMEM] * (1 + g.A),
        compiler_params=params(),
        cost_estimate=pl.CostEstimate(
            flops=g.A * g.PAIRS * g.RM * BLK * 8,
            bytes_accessed=g.A * g.PAIRS * g.RM * BLK * 6,
            transcendentals=g.A * g.PAIRS * g.RM * BLK,
        ),
        name="stats",
    )(tab, positive, *score_list)


def grad_kernel(g, groups, tab, positive, *refs):
    stats, refs = refs[: g.A], refs[g.A :]
    ng = len(groups)
    score_refs = refs[:ng]
    loss, near, far = refs[ng : ng + 3]
    others = refs[ng + 3 :]
    col = lax.broadcasted_iota(jnp.int32, (g.RM, BLK), 1)
    stats = [ref[...] for ref in stats]
    top = functools.reduce(jnp.maximum, stats)
    total = jnp.zeros((g.RM, LANES), jnp.float32)
    hit = jnp.zeros((g.RM, LANES), jnp.float32)
    for each in stats:
        total = total + pltpu.roll(each, LANES - PART, 1) * jnp.exp(each - top)
        hit = hit + pltpu.roll(each, LANES - 2 * PART, 1)
    log_total = top + jnp.log(total)
    loss[...] = log_total - hit
    for i, combos in enumerate(groups):
        for n, (s, t) in enumerate(combos):
            for c in range(g.CAP):

                def pair():
                    q = t * g.CAP + c
                    live = g.field(tab, F_LIVE, s, q)
                    first = g.field(tab, F_SLOT, s, q) == 0
                    at = g.column(tab, s, q)
                    x = score_refs[i][n * g.CAP + c] * SCORE_SCALE
                    weight = jnp.exp(x - lane_pick(log_total, at))
                    pos = lane_pick(positive[...], s * g.J + g.field(tab, F_BLOCK, s, q))
                    target = jnp.where((col == pos) & first, 1.0, 0.0)
                    grad = LOSS_SCALE * SCORE_SCALE * (weight - target)
                    grad = jnp.where(live > 0, grad, 0.0).astype(jnp.bfloat16)
                    if s == 1:
                        near[q] = grad
                    else:
                        far[g.rest(s) * g.PAIRS + q] = grad
                    if t > 0:
                        others[t - 1][s * g.CAP + c] = grad

                pair()


def grads_of(g, tab, positive, stats, score_list, groups):
    def pairs(n):
        return jax.ShapeDtypeStruct((n, g.RM, BLK), jnp.bfloat16)

    return pl.pallas_call(
        functools.partial(grad_kernel, g, groups),
        out_shape=[
            jax.ShapeDtypeStruct((g.RM, LANES), jnp.float32),
            pairs(g.PAIRS),
            pairs((g.A - 1) * g.PAIRS),
        ]
        + [pairs(g.A * g.CAP)] * (g.B - 1),
        in_specs=[SMEM, VMEM] + [VMEM] * (g.A + len(groups)),
        out_specs=[VMEM] * (g.B + 2),
        compiler_params=params(),
        cost_estimate=pl.CostEstimate(
            flops=g.A * g.PAIRS * g.RM * BLK * 8,
            bytes_accessed=g.A * g.PAIRS * g.RM * BLK * 6,
            transcendentals=g.A * g.PAIRS * g.RM * BLK,
        ),
        name="grads",
    )(tab, positive, *stats, *score_list)


def query_grad_kernel(g, s, tab, grad, *refs):
    p_refs = refs[: g.B]
    out, acc, g_buf, p_buf, g_sem, p_sem = refs[g.B :]
    base = 0 if s == 1 else g.rest(s) * g.PAIRS
    load = pltpu.make_async_copy(grad.at[:, pl.ds(base, g.PAIRS)], g_buf, g_sem)
    load.start()
    for t in range(g.B):

        def fetch(c, carry):
            at = t * g.CAP + c
            src = p_refs[t].at[g.field(tab, F_PASS, s, at)]
            pltpu.make_async_copy(src, p_buf.at[at], p_sem.at[at]).start()
            return carry

        lax.fori_loop(0, g.CAP, fetch, 0)
    acc[...] = jnp.zeros_like(acc)
    load.wait()

    def pairs(t, carry):
        for c in range(g.CAP):
            at = t * g.CAP + c
            pltpu.make_async_copy(p_refs[0].at[0], p_buf.at[at], p_sem.at[at]).wait()
            j = g.field(tab, F_BLOCK, s, at)
            rows = g_buf[:, at].reshape(g.R, BLK)
            acc[j] += jnp.dot(rows, p_buf[at], preferred_element_type=jnp.float32)
        return carry

    lax.fori_loop(0, g.B, pairs, 0)
    out[...] = acc[...].astype(out.dtype)


def query_grad_part(g, tab, grad, passages, s, dtype):
    return pl.pallas_call(
        functools.partial(query_grad_kernel, g, s),
        out_shape=jax.ShapeDtypeStruct((g.J, g.R, g.W), dtype),
        in_specs=[SMEM, ANY] + [ANY] * g.B,
        out_specs=VMEM,
        scratch_shapes=[
            pltpu.VMEM((g.J, g.R, g.W), jnp.float32),
            pltpu.VMEM((g.M, g.PAIRS, g.RM, BLK), jnp.bfloat16),
            pltpu.VMEM((g.PAIRS, BLK, g.W), jnp.bfloat16),
            pltpu.SemaphoreType.DMA,
            pltpu.SemaphoreType.DMA((g.PAIRS,)),
        ],
        compiler_params=params(),
        cost_estimate=pl.CostEstimate(
            flops=2 * g.PAIRS * g.R * BLK * g.W,
            bytes_accessed=g.PAIRS * BLK * g.W * 2 + g.J * g.R * g.W * 4,
            transcendentals=0,
        ),
        name="query_grad_part",
    )(tab, grad, *passages)


def passage_grad_kernel(g, tab, their, *refs):
    n = g.A * HALVES
    nh = 2 * HALVES
    own_g, other_g = refs[:nh], refs[nh : nh + g.B - 1]
    q_refs = refs[nh + g.B - 1 : nh + g.B - 1 + g.B * n]
    out, acc, g_buf, q_buf, others, g_sem, q_sem = refs[nh + g.B - 1 + g.B * n :]

    def copies(t, s):
        for h in range(HALVES):
            rows = pl.ds(h * g.R, g.R)
            yield pltpu.make_async_copy(
                q_refs[(t * g.A + s) * HALVES + h], q_buf.at[t % 2, s, :, rows], q_sem.at[t % 2, s, h]
            )
            for m in range(g.M):
                rows = pl.ds(h * g.R + m * g.RM, g.RM)
                if t == 0:
                    base = 0 if s == 1 else g.rest(s) * g.PAIRS
                    src = own_g[2 * h + (s != 1)].at[m, pl.ds(base, g.CAP)]
                else:
                    src = other_g[t - 1].at[m, h, pl.ds(s * g.CAP, g.CAP)]
                yield pltpu.make_async_copy(src, g_buf.at[t % 2, s, :, rows], g_sem.at[t % 2, s, h, m])

    def start(t):
        for s in range(g.A):
            for copy in copies(t, s):
                copy.start()

    start(0)
    low = their[(g.B - 1) * g.A * g.J * g.K]
    for t in range(g.B - 1):

        def listed(s, carry):
            def slot(i, found):
                name = their[((t * g.A) + s) * g.J * g.K + i] - low
                hit = (name >= 0) & (name < g.PB)

                @pl.when(hit & (found < g.CAP))
                def _():
                    others[((t * 2) * g.A + s) * g.CAP + found] = lax.div(i, g.K)
                    others[((t * 2 + 1) * g.A + s) * g.CAP + found] = name

                return found + hit.astype(jnp.int32)

            lax.fori_loop(0, g.J * g.K, slot, jnp.int32(0))
            return carry

        lax.fori_loop(0, g.A, listed, 0)
    acc[...] = jnp.zeros_like(acc)
    for t in range(g.B):
        if t + 1 < g.B:
            start(t + 1)

        def pairs(s, carry):
            for h in range(HALVES):
                half = q_buf.at[0, 0, :, pl.ds(0, g.R)]
                pltpu.make_async_copy(q_refs[0], half, q_sem.at[t % 2, s, h]).wait()
                for m in range(g.M):
                    piece = g_buf.at[0, 0, :, pl.ds(0, g.RM)]
                    src = own_g[0].at[0, pl.ds(0, g.CAP)]
                    pltpu.make_async_copy(src, piece, g_sem.at[t % 2, s, h, m]).wait()
            for c in range(g.CAP):
                if t == 0:
                    j, block = g.field(tab, F_BLOCK, s, c), g.field(tab, F_PASS, s, c)
                else:
                    j = others[(((t - 1) * 2) * g.A + s) * g.CAP + c]
                    block = others[(((t - 1) * 2 + 1) * g.A + s) * g.CAP + c]
                term = lax.dot_general(
                    g_buf[t % 2, s, c], q_buf[t % 2, s, j], (((0,), (0,)), ((), ())),
                    preferred_element_type=jnp.float32,
                )
                acc[block] += term.astype(jnp.bfloat16).astype(jnp.float32)
            return carry

        lax.fori_loop(0, g.A, pairs, 0)
    out[...] = acc[...].astype(out.dtype)


def passage_grad_of(g, tab, their, own_g, other_g, queries):
    n = g.A * HALVES
    return pl.pallas_call(
        functools.partial(passage_grad_kernel, g),
        out_shape=jax.ShapeDtypeStruct((g.PB, BLK, g.W), jnp.bfloat16),
        in_specs=[SMEM, SMEM] + [ANY] * (2 * HALVES + g.B - 1 + g.B * n),
        out_specs=VMEM,
        scratch_shapes=[
            pltpu.VMEM((g.PB, BLK, g.W), jnp.float32),
            pltpu.VMEM((min(g.B, 2), g.A, g.CAP, BLK, BLK), jnp.bfloat16),
            pltpu.VMEM((min(g.B, 2), g.A, g.J, BLK, g.W), jnp.bfloat16),
            pltpu.SMEM((max(g.B - 1, 1) * 2 * g.A * g.CAP,), jnp.int32),
            pltpu.SemaphoreType.DMA((min(g.B, 2), g.A, HALVES, g.M)),
            pltpu.SemaphoreType.DMA((min(g.B, 2), g.A, HALVES)),
        ],
        compiler_params=params(),
        cost_estimate=pl.CostEstimate(
            flops=2 * g.A * g.PAIRS * BLK * BLK * g.W,
            bytes_accessed=g.B * g.A * g.J * BLK * g.W * 2 + g.PB * BLK * g.W * 2,
            transcendentals=0,
        ),
        name="passage_grad",
    )(tab, their, *own_g, *other_g, *queries)


def place_kernel(g, where, src, out):
    def slot(i, carry):
        w = where[i]
        s, q = lax.div(w, g.PAIRS), lax.rem(w, g.PAIRS)
        for h in range(HALVES):
            out[i, pl.ds(h * g.R, g.R)] = src[:, h, s, q].reshape(g.R, BLK)
        return carry

    lax.fori_loop(0, g.J * g.K, slot, 0)


def place(g, where, gathered):
    return pl.pallas_call(
        functools.partial(place_kernel, g),
        out_shape=jax.ShapeDtypeStruct((g.J * g.K, BLK, BLK), jnp.bfloat16),
        in_specs=[SMEM, VMEM],
        out_specs=VMEM,
        compiler_params=params(),
        cost_estimate=pl.CostEstimate(
            flops=0, bytes_accessed=2 * g.J * g.K * BLK * BLK * 2, transcendentals=0
        ),
        name="place",
    )(where, gathered)


def grid_of(count):
    cols = 2 ** (int(math.log2(count)) // 2)
    return count // cols, cols


def shards(query_emb, passage_emb, block_ids, list_len, positive):
    count = lax.axis_size("dp")
    rows, cols = grid_of(count)
    width = query_emb.shape[1]
    g = Plan(
        rows, cols, lax.axis_size("mp"), block_ids.shape[0], block_ids.shape[1],
        passage_emb.shape[0] // BLK, width,
    )
    A, B, J, K = g.A, g.B, g.J, g.K
    ring = [(a * B + b, (a + 1) % A * B + b) for a in range(A) for b in range(B)]

    def back(s):
        return [(a * B + b, (a - s) % A * B + b) for a in range(A) for b in range(B)]

    def turn(t):
        return [(a * B + b, a * B + (b + t) % B) for a in range(A) for b in range(B)]

    me = lax.axis_index("dp")
    row, column = me // B, me % B

    own_q = query_emb.reshape(J, HALVES, g.R, width)
    own_p = passage_emb.reshape(g.PB, BLK, width)
    passages = [own_p]
    for t in range(1, B):
        passages.append(lax.ppermute(own_p, "dp", turn(B - t)))
    info = [jnp.concatenate([block_ids, list_len[:, None], positive.reshape(J, BLK)], axis=1)]
    for s in range(1, A):
        info.append(lax.ppermute(info[0], "dp", back(A - s)))
    info = jnp.stack(info)
    queries = []
    held = None
    for h in range(HALVES):
        now = own_q[:, h]
        if held is not None:
            now, _ = lax.optimization_barrier((now, held))
        ringed = [now]
        for _ in range(1, A):
            ringed.append(lax.ppermute(ringed[-1], "dp", ring))
        held = ringed[-1]
        queries.append(ringed)
    other_q = []
    for t in range(1, B):
        part = []
        for s in range(A):
            for h in range(HALVES):
                src, _ = lax.optimization_barrier((queries[h][s], passages[-1]))
                part.append(lax.ppermute(src, "dp", turn(B - t)))
        other_q.append(part)

    ids = info[:, :, :K].reshape(A, J * K)
    lens = info[:, :, K]
    owner = ids // g.PB
    order = jnp.arange(J * K, dtype=jnp.int32)

    def rank_of(owner):
        same = (owner[:, :, None] == owner[:, None, :]) & (order[None, None, :] < order[None, :, None])
        return jnp.sum(same.astype(jnp.int32), axis=2)

    def pick(values):
        return jnp.sum(jnp.where(hot, values[:, None, :], 0), axis=2)

    slot_block = jnp.broadcast_to(order // K, ids.shape)
    place_of = (owner % B + B - column) % B * g.CAP + rank_of(owner)
    mine = jnp.where(owner // B == row, place_of, -1)
    hot = mine[:, None, :] == jnp.arange(g.PAIRS, dtype=jnp.int32)[None, :, None]
    live = order[None, :] % K < jnp.repeat(lens, K, axis=1)
    fields = [
        pick(slot_block),
        pick(jnp.broadcast_to(order % K, ids.shape)),
        pick(live.astype(jnp.int32)),
        pick(ids % g.PB),
    ]
    tab = jnp.concatenate([jnp.stack(fields).reshape(-1), row.reshape(1)])
    where = (owner[0] // B + A - row) % A * g.PAIRS + place_of[0]
    their = []
    for t in range(1, B):
        names, _ = lax.optimization_barrier((ids, passages[-1]))
        their.append(lax.ppermute(names, "dp", turn(B - t)).reshape(-1))
    their = jnp.concatenate([*their, (me * g.PB).reshape(1)])

    m = lax.axis_index("mp")
    lanes = info[:, :, K + 1 :].reshape(A * J, HALVES, g.M, g.RM)
    lanes = lax.dynamic_index_in_dim(lanes, m, 2, keepdims=False).transpose(1, 2, 0)
    lanes = jnp.pad(lanes, ((0, 0), (0, 0), (0, LANES - A * J)))

    grads, losses, seen, sent = [], [], [], []
    for h in range(HALVES):
        if h == 0 and HALVES > 1:
            first = [(s, 0) for s in range(A - 1)]
        else:
            first = [(s, t) for t in range(B) for s in range(A - 1)]
        rest = [(s, t) for t in range(B) for s in range(A) if (s, t) not in first]
        groups = [first, rest]
        score_list = []
        for combos in groups:
            part = scores(g, tab, queries[h], passages, combos)
            score_list.append(lax.psum_scatter(part, "mp", scatter_dimension=0))
        stats, *shown = stats_of(g, tab, lanes[h], score_list, groups)
        joined = [stats]
        for s in range(1, A):
            joined.append(lax.ppermute(stats, "dp", back(s)))
        loss, near, rest, *crossing = grads_of(g, tab, lanes[h], joined, score_list, groups)
        near = lax.all_gather(near, "mp")
        rest = lax.all_gather(rest, "mp")
        grads.append((near, rest))
        got = []
        for t in range(1, B):
            got.append(lax.ppermute(crossing[t - 1], "dp", turn(t)))
        sent.append(got)
        losses.append(loss)
        took = [shown[0]]
        for s in range(1, A):
            took.append(lax.ppermute(shown[s], "dp", back(s)))
        seen.append(took)

    out_q = []
    for h in range(HALVES):
        total = query_grad_part(g, tab, grads[h][0], passages, 1, jnp.bfloat16)
        for s in [*range(2, A), 0]:
            part = query_grad_part(g, tab, grads[h][1], passages, s, jnp.float32)
            total = lax.ppermute(total, "dp", ring)
            total = (part + total.astype(jnp.float32)).astype(jnp.bfloat16)
        out_q.append(total)
    query_grad = jnp.stack(out_q, axis=1).reshape(J * BLK, width)

    own_g = [part for h in range(HALVES) for part in grads[h]]
    other_g = []
    for t in range(1, B):
        both = jnp.stack([sent[h][B - t - 1] for h in range(HALVES)])
        other_g.append(lax.all_gather(both, "mp"))
    flat_q = [queries[h][s] for s in range(A) for h in range(HALVES)]
    for part in other_q:
        flat_q += part
    passage_grad = passage_grad_of(g, tab, their, own_g, other_g, flat_q)
    passage_grad = passage_grad.reshape(g.PB * BLK, width)

    shown = jnp.stack([jnp.stack(part) for part in seen])
    shown = lax.all_gather(shown, "mp")
    block_scores = place(g, where, shown).reshape(J, K, BLK, BLK)
    loss = lax.dynamic_slice_in_dim(jnp.stack(losses), row * J, J, 2)
    loss = lax.all_gather(loss, "mp")
    query_loss = loss.transpose(3, 1, 0, 2).reshape(J * BLK)
    return block_scores, query_loss, query_grad, passage_grad


def solution(mesh):
    return jax.shard_map(
        shards,
        mesh=mesh,
        in_specs=(P("dp", "mp"), P("dp", "mp"), P("dp", None), P("dp"), P("dp")),
        out_specs=(P("dp", None, None, None), P("dp"), P("dp", "mp"), P("dp", "mp")),
        check_vma=False,
    )
```
